32 devices in a mesh: seq: 4 (over z), chan: 4 (over y, core), rep: 2 (over x).
Axes of the slice: x: 2, y: 2, z: 4, core: 2. Of those that a mesh axis runs over, the one named last changes fastest.
Arguments:
- inputs: float32 [2, 4096, 512], P('rep', 'chan', 'seq'), may hold values from -0.25 to 0.25
- out_grad: float32 [2, 4096, 512], P('rep', 'chan', 'seq'), may hold values from -6 to 6
- filters: float32 [4, 1024, 512], P('chan', 'seq'), may hold values from -0.25 to 0.25
- segment_ids: int32 [2, 512], P('rep'), may hold values from 0 to 1, as said below
Outputs:
- input_grad: float32 [2, 4096, 512], P('rep', 'chan', 'seq')
- filter_grad: float32 [4, 1024, 512], P('chan', 'seq')
The draws below stay inside these ranges and needn't reach their ends.
Inputs may be any that keep to these rules, and one draw needn't show every extreme that they name: `segment_ids`: in each replica's row the ids are 0 up to some position and 1 from it on; that position lies between 64 and 448.
All inputs are finite; a program needn't handle non-finite values.
Results may differ from the reference program's by a relative error of at most 0.000098.
Values sent between devices are 32-bit elements; how exact they have to be, the bound alone decides.
A program may use at most 64 MiB of HBM per device.

```python
import jax
import jax.numpy as jnp
from jax import lax

CHANNELS = 4096
L = 512
REPS = 2
SLABS = 4
SLAB = 1024


def draw_segment_ids(key, part):
    cutoff = jax.random.randint(key, (REPS, 1), L // 8, L - L // 8 + 1)
    position = jnp.arange(L, dtype=jnp.int32)[None, :]
    return (position >= cutoff).astype(jnp.int32)


def level_of(key, extent, split, low, high):
    level, own = 1.0, jax.random.fold_in(key, 6)
    for dim, parts in split:
        steps = jnp.exp(jax.random.uniform(jax.random.fold_in(own, dim), (parts,), jnp.float32, low / len(split), high / len(split)))
        level = level * jnp.repeat(steps, extent[dim] // parts).reshape([-1 if axis == dim else 1 for axis in range(len(extent))])
    return level


def centred(own_key, extent, deviation, limit, shards=(), held_as=jnp.bfloat16):
    values = deviation * jax.random.normal(own_key, extent, jnp.float32)
    if shards:
        values = values * level_of(own_key, extent, shards, -0.22, 0.18)
    return jnp.clip(values, -limit, limit).astype(held_as)


def setup_inputs(seed: int = 0) -> dict:
    keys = jax.random.split(jax.random.key(seed), 5)
    return {
        "inputs": centred(keys[0], (REPS, CHANNELS, L), L ** -0.5, 0.25, ((0, 2), (1, 4), (2, 4)), jnp.float32),
        "out_grad": centred(keys[1], (REPS, CHANNELS, L), 1.0, 6.0, ((0, 2), (1, 4), (2, 4)), jnp.float32),
        "filters": centred(keys[2], (SLABS, SLAB, L), L ** -0.5, 0.25, ((0, 4), (1, 4)), jnp.float32),
        "segment_ids": draw_segment_ids(jax.random.fold_in(keys[4], 71), 0),
    }


def block_grads(act_block, grad_block, filt_block, second_mask):
    full_len = 2 * L
    first_mask = 1.0 - second_mask
    first_rows = first_mask[:, None, :]
    second_rows = second_mask[:, None, :]
    filt_spec = jnp.fft.rfft(filt_block, n=full_len)
    grad_first = jnp.fft.rfft(grad_block * first_rows, n=full_len)
    grad_second = jnp.fft.rfft(grad_block * second_rows, n=full_len)
    act_first = jnp.fft.rfft(act_block * first_rows, n=full_len)
    act_second = jnp.fft.rfft(act_block * second_rows, n=full_len)
    back_first = jnp.fft.irfft(jnp.conj(filt_spec)[None] * grad_first, n=full_len)[..., :L]
    back_second = jnp.fft.irfft(jnp.conj(filt_spec)[None] * grad_second, n=full_len)[..., :L]
    input_part = first_rows * back_first + second_rows * back_second
    filt_grad = jnp.fft.irfft(jnp.conj(act_first) * grad_first + jnp.conj(act_second) * grad_second, n=full_len)[..., :L]
    return input_part, jnp.sum(filt_grad, axis=0)


def reference(inputs, out_grad, filters, segment_ids):
    second_mask = segment_ids.astype(jnp.float32)
    block_width = 128 if CHANNELS % 128 == 0 else CHANNELS
    block_count = CHANNELS // block_width
    act_blocks = inputs.reshape(REPS, block_count, block_width, L).transpose(1, 0, 2, 3)
    grad_blocks = out_grad.reshape(REPS, block_count, block_width, L).transpose(1, 0, 2, 3)
    filt_blocks = filters.reshape(block_count, block_width, L)

    def run_block(block_args):
        return block_grads(block_args[0], block_args[1], block_args[2], second_mask)

    input_parts, filt_parts = lax.map(run_block, (act_blocks, grad_blocks, filt_blocks))
    input_grad = input_parts.transpose(1, 0, 2, 3).reshape(REPS, CHANNELS, L)
    filter_grad = filt_parts.reshape(SLABS, SLAB, L)
    return input_grad, filter_grad
```

```python
import functools
import math

import jax
import jax.numpy as jnp
import numpy as np
from jax import lax
from jax.experimental import pallas as pl
from jax.experimental.pallas import tpu as pltpu
from jax.sharding import PartitionSpec as P

MESH = pl.DeviceIdType.MESH
TABLE_BYTES = 8 << 20
CHUNKS = 2


def table_pair(row_count, col_count, period):
    row_index = jnp.arange(row_count, dtype=jnp.int32)[:, None]
    col_index = jnp.arange(col_count, dtype=jnp.int32)[None, :]
    phases = row_index * col_index % period
    angles = phases.astype(jnp.float32) * (2.0 * math.pi / period)
    return (jnp.cos(angles), -jnp.sin(angles))


def contract(formula, left_part, right_part):
    return jnp.einsum(
        formula,
        left_part,
        right_part,
        precision=lax.Precision.HIGHEST,
        preferred_element_type=jnp.float32,
    )


def make_tables(length):
    full_len = 2 * length
    col_size = 128
    row_size = full_len // col_size
    half_rows = row_size // 2
    outer_cos, outer_sin = table_pair(row_size, row_size, row_size)
    fwd_cos = outer_cos[:, :half_rows]
    fwd_sin = outer_sin[:, :half_rows]
    outer_fwd = jnp.concatenate(
        [jnp.concatenate([fwd_cos, -fwd_sin], axis=1), jnp.concatenate([fwd_sin, fwd_cos], axis=1)],
        axis=0,
    )
    inv_cos = outer_cos[:half_rows]
    inv_sin = outer_sin[:half_rows]
    outer_inv = jnp.concatenate(
        [jnp.concatenate([inv_cos, inv_sin], axis=1), jnp.concatenate([-inv_sin, inv_cos], axis=1)],
        axis=0,
    )
    twiddle = table_pair(row_size, col_size, full_len)
    inner_cos, inner_sin = table_pair(col_size, col_size, col_size)
    inner_fwd = jnp.stack(
        [jnp.stack([inner_cos, inner_sin], axis=1), jnp.stack([-inner_sin, inner_cos], axis=1)],
        axis=0,
    )
    inner_inv = jnp.stack(
        [jnp.stack([inner_cos, -inner_sin], axis=1), jnp.stack([inner_sin, inner_cos], axis=1)],
        axis=0,
    )
    return (outer_fwd, outer_inv, twiddle, inner_fwd, inner_inv, half_rows, col_size)


def forward_spectrum(signal, real_only, tables):
    outer_fwd, outer_inv, twiddle, inner_fwd, inner_inv, half_rows, col_size = tables
    chan_count = signal.shape[0]
    if real_only:
        section = contract("ja,cab->cjb", outer_fwd[:, :half_rows], signal)
    else:
        section = contract(
            "ja,cab->cjb", outer_fwd, signal.reshape(chan_count, 2 * half_rows, col_size)
        )
    section = section.reshape(chan_count, 2, 2 * half_rows, col_size)
    section_re = section[:, 0]
    section_im = section[:, 1]
    turned = jnp.stack(
        [
            section_re * twiddle[0] - section_im * twiddle[1],
            section_re * twiddle[1] + section_im * twiddle[0],
        ],
        axis=1,
    )
    return contract("cpjb,pbqm->cqjm", turned, inner_fwd)


def inverse_signal(spectrum, tables, want_imag):
    outer_fwd, outer_inv, twiddle, inner_fwd, inner_inv, half_rows, col_size = tables
    chan_count = spectrum.shape[0]
    factor = 1.0 / (2 * half_rows * col_size)
    mixed = contract("cqjm,qmpb->cpjb", spectrum, inner_inv)
    mixed_re = mixed[:, 0]
    mixed_im = mixed[:, 1]
    turned = jnp.stack(
        [
            mixed_re * twiddle[0] + mixed_im * twiddle[1],
            mixed_im * twiddle[0] - mixed_re * twiddle[1],
        ],
        axis=1,
    )
    turned = turned.reshape(chan_count, 4 * half_rows, col_size)
    table = outer_inv if want_imag else outer_inv[:half_rows]
    signal = contract("aj,cjb->cab", table, turned) * factor
    return signal.reshape(chan_count, -1, half_rows, col_size)


def conj_product(left_spec, right_spec):
    left_re = left_spec[:, 0]
    left_im = left_spec[:, 1]
    right_re = right_spec[:, 0]
    right_im = right_spec[:, 1]
    return jnp.stack(
        [left_re * right_re + left_im * right_im, left_re * right_im - left_im * right_re], axis=1
    )


def pair_spectrum(whole, first_mask, second_mask, tables):
    signal = whole.reshape(-1, tables[5], tables[6])
    packed = jnp.stack([signal * first_mask, signal * second_mask], axis=1)
    return forward_spectrum(packed, False, tables)


def return_grad(filter_spec, grad_spec, first_mask, second_mask, tables, slab_width, tok_count):
    product = conj_product(filter_spec, grad_spec)
    back = inverse_signal(product, tables, True)
    grad_full = first_mask * back[:, 0] + second_mask * back[:, 1]
    chan_count = grad_full.shape[0]
    pieces = grad_full.reshape(1, chan_count, -1)
    returned = lax.all_to_all(pieces, "seq", split_axis=2, concat_axis=0, tiled=True)
    return returned.reshape(1, slab_width, tok_count)


def sum_filter_grad(act_spec, grad_spec, tables):
    product = conj_product(act_spec, grad_spec)
    signal_re = inverse_signal(product, tables, False)
    chan_count = signal_re.shape[0]
    return lax.psum(signal_re.reshape(1, chan_count, -1), "rep")


def long_body(inputs, out_grad, filters, segment_ids):
    seq_count = lax.axis_size("seq")
    slab_width = inputs.shape[1]
    tok_count = inputs.shape[2]
    chan_count = slab_width // seq_count
    length = tok_count * seq_count
    tables = make_tables(length)
    half_rows = tables[5]
    col_size = tables[6]
    second_mask = segment_ids[0].astype(jnp.float32).reshape(half_rows, col_size)
    first_mask = 1.0 - second_mask
    filter_spec = forward_spectrum(
        filters[0].reshape(chan_count, half_rows, col_size), True, tables
    )
    act_pieces = inputs.reshape(seq_count, chan_count, tok_count)
    grad_pieces = out_grad.reshape(seq_count, chan_count, tok_count)
    act_whole, grad_whole = (
        lax.all_to_all(act_pieces, "seq", split_axis=0, concat_axis=2, tiled=True),
        lax.all_to_all(grad_pieces, "seq", split_axis=0, concat_axis=2, tiled=True),
    )
    grad_spec = pair_spectrum(grad_whole, first_mask, second_mask, tables)
    input_grad = return_grad(
        filter_spec, grad_spec, first_mask, second_mask, tables, slab_width, tok_count
    )
    act_spec = pair_spectrum(act_whole, first_mask, second_mask, tables)
    filter_grad = sum_filter_grad(act_spec, grad_spec, tables)
    return (input_grad, filter_grad)


def dense_table(length):
    phase = np.arange(length)[:, None] * (2 * np.arange(length)[None, :] + 1) % (4 * length)
    angle = phase * (math.pi / (2 * length))
    table = np.concatenate([np.cos(angle), -np.sin(angle)], axis=1).astype(np.float32)
    high = table.astype(jnp.bfloat16)
    low = (table - high.astype(np.float32)).astype(jnp.bfloat16)
    return high, low


def split(value):
    high = value.astype(jnp.bfloat16)
    low = (value - high.astype(jnp.float32)).astype(jnp.bfloat16)
    return high, low


def dot(left, right, inverse):
    dims = (((1,), (1 if inverse else 0,)), ((), ()))
    return lax.dot_general(left, right, dims, preferred_element_type=jnp.float32)


def triple(high, low, high_table, low_table, inverse):
    return dot(high, high_table, inverse) + (
        dot(low, high_table, inverse) + dot(high, low_table, inverse)
    )


def conj_mul(left, right, bins):
    left_re, left_im = left[:, :bins], left[:, bins:]
    right_re, right_im = right[:, :bins], right[:, bins:]
    return jnp.concatenate(
        [left_re * right_re + left_im * right_im, left_re * right_im - left_im * right_re], axis=1
    )


def kernel(
    seqs, reps, chunks,
    act_hbm, grad_hbm, filt_hbm, seg_ref, high_hbm, low_hbm,
    back_hbm, fgrad_hbm,
    act_buf, grad_buf, filt_buf, high_buf, low_buf, spec_buf, ret_buf, part_buf, sum_buf,
    in_send, in_recv, ret_send, ret_recv, part_send, part_recv, own_sem, load_sem, out_sem, fin_sem,
):
    me = lax.axis_index("seq")
    rep = lax.axis_index("rep")
    _, chans, toks = act_buf.shape
    length = seqs * toks
    bins = length
    rows = chans // chunks

    loads = [
        pltpu.make_async_copy(filt_hbm, filt_buf, load_sem.at[0]),
        pltpu.make_async_copy(high_hbm, high_buf, load_sem.at[1]),
        pltpu.make_async_copy(low_hbm, low_buf, load_sem.at[2]),
    ]
    own = pl.ds(pl.multiple_of(me * chans, chans), chans)
    owns = [
        pltpu.make_async_copy(grad_hbm.at[own], grad_buf.at[me], own_sem.at[0]),
        pltpu.make_async_copy(act_hbm.at[own], act_buf.at[me], own_sem.at[1]),
    ]
    for copy in loads + owns:
        copy.start()

    barrier = pltpu.get_barrier_semaphore()
    for dist in range(1, seqs):
        pl.semaphore_signal(
            barrier, inc=1, device_id={"seq": lax.rem(me + dist, seqs)}, device_id_type=MESH
        )
    for dist in range(1, reps):
        pl.semaphore_signal(
            barrier, inc=1, device_id={"rep": lax.rem(rep + dist, reps)}, device_id_type=MESH
        )
    pl.semaphore_wait(barrier, seqs - 1 + reps - 1)

    arrivals = []
    for chunk in range(chunks):
        for kind, (source, target) in enumerate(((grad_hbm, grad_buf), (act_hbm, act_buf))):
            group = []
            for dist in range(1, seqs):
                peer = lax.rem(me + dist, seqs)
                first = pl.multiple_of(peer * chans + chunk * rows, rows)
                copy = pltpu.make_async_remote_copy(
                    src_ref=source.at[pl.ds(first, rows)],
                    dst_ref=target.at[me, pl.ds(chunk * rows, rows)],
                    send_sem=in_send.at[chunk, kind, dist - 1],
                    recv_sem=in_recv.at[chunk, kind, dist - 1],
                    device_id={"seq": peer},
                    device_id_type=MESH,
                )
                copy.start()
                group.append(copy)
            arrivals.append(group)

    second = seg_ref[...].astype(jnp.float32)
    first_mask = 1.0 - second
    second_bf = second.astype(jnp.bfloat16)
    first_bf = first_mask.astype(jnp.bfloat16)

    for copy in loads:
        copy.wait()
    high, low = split(filt_buf[...])
    spec_buf[...] = triple(high, low, high_buf[...], low_buf[...], False)

    def pair_spectrum(buf, chunk):
        whole = jnp.concatenate(
            [buf[seq, pl.ds(chunk * rows, rows), :] for seq in range(seqs)], axis=1
        )
        high, low = split(whole)
        highs = jnp.concatenate([high * first_bf, high * second_bf], axis=0)
        lows = jnp.concatenate([low * first_bf, low * second_bf], axis=0)
        return triple(highs, lows, high_buf[...], low_buf[...], False)

    def inverse(spectrum):
        high, low = split(spectrum)
        return triple(high, low, high_buf[...], low_buf[...], True) * (1.0 / length)

    returns = []
    parts = []
    for chunk in range(chunks):
        span = pl.ds(chunk * rows, rows)
        if chunk == 0:
            owns[0].wait()
        for copy in arrivals[2 * chunk]:
            copy.wait_recv()
        grad_spec = pair_spectrum(grad_buf, chunk)
        filt_spec = spec_buf[span, :]
        both = jnp.concatenate(
            [conj_mul(filt_spec, grad_spec[:rows], bins), conj_mul(filt_spec, grad_spec[rows:], bins)],
            axis=0,
        )
        back = inverse(both)
        back = first_mask * back[:rows] + second * back[rows:]
        for seq in range(seqs):
            ret_buf[seq, span, :] = back[:, seq * toks : (seq + 1) * toks]
        target = pl.ds(pl.multiple_of(me * chans + chunk * rows, rows), rows)
        for dist in range(1, seqs):
            peer = lax.rem(me + dist, seqs)
            copy = pltpu.make_async_remote_copy(
                src_ref=ret_buf.at[peer, span],
                dst_ref=back_hbm.at[target],
                send_sem=ret_send.at[chunk, dist - 1],
                recv_sem=ret_recv.at[chunk, dist - 1],
                device_id={"seq": peer},
                device_id_type=MESH,
            )
            copy.start()
            returns.append(copy)
        keep = pltpu.make_async_copy(ret_buf.at[me, span], back_hbm.at[target], out_sem.at[chunk])
        keep.start()
        returns.append(keep)

        if chunk == 0:
            owns[1].wait()
        for copy in arrivals[2 * chunk + 1]:
            copy.wait_recv()
        act_spec = pair_spectrum(act_buf, chunk)
        total = conj_mul(act_spec[:rows], grad_spec[:rows], bins) + conj_mul(
            act_spec[rows:], grad_spec[rows:], bins
        )
        part_buf[rep, span, :] = inverse(total)
        for dist in range(1, reps):
            copy = pltpu.make_async_remote_copy(
                src_ref=part_buf.at[rep, span],
                dst_ref=part_buf.at[rep, span],
                send_sem=part_send.at[chunk, dist - 1],
                recv_sem=part_recv.at[chunk, dist - 1],
                device_id={"rep": lax.rem(rep + dist, reps)},
                device_id_type=MESH,
            )
            copy.start()
            parts.append(copy)

    stores = []
    for chunk in range(chunks):
        span = pl.ds(chunk * rows, rows)
        for copy in parts[chunk * (reps - 1) : (chunk + 1) * (reps - 1)]:
            copy.wait()
        total = part_buf[0, span, :]
        for other in range(1, reps):
            total = total + part_buf[other, span, :]
        sum_buf[span, :] = total
        store = pltpu.make_async_copy(sum_buf.at[span], fgrad_hbm.at[span], fin_sem.at[chunk])
        store.start()
        stores.append(store)
    for group in arrivals:
        for copy in group:
            copy.wait_send()
    for copy in returns + stores:
        copy.wait()


def dense_body(inputs, out_grad, filters, segment_ids):
    seqs = lax.axis_size("seq")
    reps = lax.axis_size("rep")
    slab, toks = inputs.shape[1:]
    chans = slab // seqs
    length = seqs * toks
    chunks = CHUNKS
    rows = chans // chunks
    high, low = dense_table(length)
    anywhere = pl.BlockSpec(memory_space=pl.ANY)
    vmem = pl.BlockSpec(memory_space=pltpu.VMEM)
    f32, bf16, dma = jnp.float32, jnp.bfloat16, pltpu.SemaphoreType.DMA
    back, fgrad = pl.pallas_call(
        functools.partial(kernel, seqs, reps, chunks),
        out_shape=(
            jax.ShapeDtypeStruct((slab, toks), f32),
            jax.ShapeDtypeStruct((chans, length), f32),
        ),
        in_specs=[anywhere] * 3 + [vmem] + [anywhere] * 2,
        out_specs=(anywhere, anywhere),
        scratch_shapes=[
            pltpu.VMEM((seqs, chans, toks), f32),
            pltpu.VMEM((seqs, chans, toks), f32),
            pltpu.VMEM((chans, length), f32),
            pltpu.VMEM((length, 2 * length), bf16),
            pltpu.VMEM((length, 2 * length), bf16),
            pltpu.VMEM((chans, 2 * length), f32),
            pltpu.VMEM((seqs, chans, toks), f32),
            pltpu.VMEM((reps, chans, length), f32),
            pltpu.VMEM((chans, length), f32),
            dma((chunks, 2, seqs - 1)),
            dma((chunks, 2, seqs - 1)),
            dma((chunks, seqs - 1)),
            dma((chunks, seqs - 1)),
            dma((chunks, reps - 1)),
            dma((chunks, reps - 1)),
            dma((2,)),
            dma((3,)),
            dma((chunks,)),
            dma((chunks,)),
        ],
        compiler_params=pltpu.CompilerParams(
            collective_id=0, has_side_effects=True, vmem_limit_bytes=60000 * 1024
        ),
    )(inputs[0], out_grad[0], filters[0], segment_ids, jnp.asarray(high), jnp.asarray(low))
    return back[None], fgrad[None]


def body(inputs, out_grad, filters, segment_ids):
    length = filters.shape[2]
    if length * 2 * length * 4 <= TABLE_BYTES:
        return dense_body(inputs, out_grad, filters, segment_ids)
    return long_body(inputs, out_grad, filters, segment_ids)


def solution(mesh):
    return jax.shard_map(
        body,
        mesh=mesh,
        in_specs=(
            P("rep", "chan", "seq"),
            P("rep", "chan", "seq"),
            P("chan", "seq", None),
            P("rep", None),
        ),
        out_specs=(P("rep", "chan", "seq"), P("chan", "seq", None)),
        check_vma=False,
    )
```

```python
import functools
import math

import jax
import jax.numpy as jnp
import numpy as np
from jax import lax
from jax.experimental import pallas as pl
from jax.experimental.pallas import tpu as pltpu
from jax.sharding import PartitionSpec as P

MESH = pl.DeviceIdType.MESH
TABLE_BYTES = 8 << 20
CHUNKS = 4


def table_pair(row_count, col_count, period):
    row_index = jnp.arange(row_count, dtype=jnp.int32)[:, None]
    col_index = jnp.arange(col_count, dtype=jnp.int32)[None, :]
    phases = row_index * col_index % period
    angles = phases.astype(jnp.float32) * (2.0 * math.pi / period)
    return (jnp.cos(angles), -jnp.sin(angles))


def contract(formula, left_part, right_part):
    return jnp.einsum(
        formula,
        left_part,
        right_part,
        precision=lax.Precision.HIGHEST,
        preferred_element_type=jnp.float32,
    )


def make_tables(length):
    full_len = 2 * length
    col_size = 128
    row_size = full_len // col_size
    half_rows = row_size // 2
    outer_cos, outer_sin = table_pair(row_size, row_size, row_size)
    fwd_cos = outer_cos[:, :half_rows]
    fwd_sin = outer_sin[:, :half_rows]
    outer_fwd = jnp.concatenate(
        [jnp.concatenate([fwd_cos, -fwd_sin], axis=1), jnp.concatenate([fwd_sin, fwd_cos], axis=1)],
        axis=0,
    )
    inv_cos = outer_cos[:half_rows]
    inv_sin = outer_sin[:half_rows]
    outer_inv = jnp.concatenate(
        [jnp.concatenate([inv_cos, inv_sin], axis=1), jnp.concatenate([-inv_sin, inv_cos], axis=1)],
        axis=0,
    )
    twiddle = table_pair(row_size, col_size, full_len)
    inner_cos, inner_sin = table_pair(col_size, col_size, col_size)
    inner_fwd = jnp.stack(
        [jnp.stack([inner_cos, inner_sin], axis=1), jnp.stack([-inner_sin, inner_cos], axis=1)],
        axis=0,
    )
    inner_inv = jnp.stack(
        [jnp.stack([inner_cos, -inner_sin], axis=1), jnp.stack([inner_sin, inner_cos], axis=1)],
        axis=0,
    )
    return (outer_fwd, outer_inv, twiddle, inner_fwd, inner_inv, half_rows, col_size)


def forward_spectrum(signal, real_only, tables):
    outer_fwd, outer_inv, twiddle, inner_fwd, inner_inv, half_rows, col_size = tables
    chan_count = signal.shape[0]
    if real_only:
        section = contract("ja,cab->cjb", outer_fwd[:, :half_rows], signal)
    else:
        section = contract(
            "ja,cab->cjb", outer_fwd, signal.reshape(chan_count, 2 * half_rows, col_size)
        )
    section = section.reshape(chan_count, 2, 2 * half_rows, col_size)
    section_re = section[:, 0]
    section_im = section[:, 1]
    turned = jnp.stack(
        [
            section_re * twiddle[0] - section_im * twiddle[1],
            section_re * twiddle[1] + section_im * twiddle[0],
        ],
        axis=1,
    )
    return contract("cpjb,pbqm->cqjm", turned, inner_fwd)


def inverse_signal(spectrum, tables, want_imag):
    outer_fwd, outer_inv, twiddle, inner_fwd, inner_inv, half_rows, col_size = tables
    chan_count = spectrum.shape[0]
    factor = 1.0 / (2 * half_rows * col_size)
    mixed = contract("cqjm,qmpb->cpjb", spectrum, inner_inv)
    mixed_re = mixed[:, 0]
    mixed_im = mixed[:, 1]
    turned = jnp.stack(
        [
            mixed_re * twiddle[0] + mixed_im * twiddle[1],
            mixed_im * twiddle[0] - mixed_re * twiddle[1],
        ],
        axis=1,
    )
    turned = turned.reshape(chan_count, 4 * half_rows, col_size)
    table = outer_inv if want_imag else outer_inv[:half_rows]
    signal = contract("aj,cjb->cab", table, turned) * factor
    return signal.reshape(chan_count, -1, half_rows, col_size)


def conj_product(left_spec, right_spec):
    left_re = left_spec[:, 0]
    left_im = left_spec[:, 1]
    right_re = right_spec[:, 0]
    right_im = right_spec[:, 1]
    return jnp.stack(
        [left_re * right_re + left_im * right_im, left_re * right_im - left_im * right_re], axis=1
    )


def pair_spectrum(whole, first_mask, second_mask, tables):
    signal = whole.reshape(-1, tables[5], tables[6])
    packed = jnp.stack([signal * first_mask, signal * second_mask], axis=1)
    return forward_spectrum(packed, False, tables)


def return_grad(filter_spec, grad_spec, first_mask, second_mask, tables, slab_width, tok_count):
    product = conj_product(filter_spec, grad_spec)
    back = inverse_signal(product, tables, True)
    grad_full = first_mask * back[:, 0] + second_mask * back[:, 1]
    chan_count = grad_full.shape[0]
    pieces = grad_full.reshape(1, chan_count, -1)
    returned = lax.all_to_all(pieces, "seq", split_axis=2, concat_axis=0, tiled=True)
    return returned.reshape(1, slab_width, tok_count)


def sum_filter_grad(act_spec, grad_spec, tables):
    product = conj_product(act_spec, grad_spec)
    signal_re = inverse_signal(product, tables, False)
    chan_count = signal_re.shape[0]
    return lax.psum(signal_re.reshape(1, chan_count, -1), "rep")


def long_body(inputs, out_grad, filters, segment_ids):
    seq_count = lax.axis_size("seq")
    slab_width = inputs.shape[1]
    tok_count = inputs.shape[2]
    chan_count = slab_width // seq_count
    length = tok_count * seq_count
    tables = make_tables(length)
    half_rows = tables[5]
    col_size = tables[6]
    second_mask = segment_ids[0].astype(jnp.float32).reshape(half_rows, col_size)
    first_mask = 1.0 - second_mask
    filter_spec = forward_spectrum(
        filters[0].reshape(chan_count, half_rows, col_size), True, tables
    )
    act_pieces = inputs.reshape(seq_count, chan_count, tok_count)
    grad_pieces = out_grad.reshape(seq_count, chan_count, tok_count)
    act_whole, grad_whole = (
        lax.all_to_all(act_pieces, "seq", split_axis=0, concat_axis=2, tiled=True),
        lax.all_to_all(grad_pieces, "seq", split_axis=0, concat_axis=2, tiled=True),
    )
    grad_spec = pair_spectrum(grad_whole, first_mask, second_mask, tables)
    input_grad = return_grad(
        filter_spec, grad_spec, first_mask, second_mask, tables, slab_width, tok_count
    )
    act_spec = pair_spectrum(act_whole, first_mask, second_mask, tables)
    filter_grad = sum_filter_grad(act_spec, grad_spec, tables)
    return (input_grad, filter_grad)


def dense_table(length):
    phase = np.arange(length)[:, None] * (2 * np.arange(length)[None, :] + 1) % (4 * length)
    angle = phase * (math.pi / (2 * length))
    table = np.concatenate([np.cos(angle), -np.sin(angle)], axis=1).astype(np.float32)
    high = table.astype(jnp.bfloat16)
    low = (table - high.astype(np.float32)).astype(jnp.bfloat16)
    return high, low


def split(value):
    high = value.astype(jnp.bfloat16)
    low = (value - high.astype(jnp.float32)).astype(jnp.bfloat16)
    return high, low


def dot(left, right, inverse):
    dims = (((1,), (1 if inverse else 0,)), ((), ()))
    return lax.dot_general(left, right, dims, preferred_element_type=jnp.float32)


def triple(high, low, high_table, low_table, inverse):
    return dot(high, high_table, inverse) + (
        dot(low, high_table, inverse) + dot(high, low_table, inverse)
    )


def conj_mul(left, right, bins):
    left_re, left_im = left[:, :bins], left[:, bins:]
    right_re, right_im = right[:, :bins], right[:, bins:]
    return jnp.concatenate(
        [left_re * right_re + left_im * right_im, left_re * right_im - left_im * right_re], axis=1
    )


def kernel(
    seqs, reps, chunks,
    act_hbm, grad_hbm, filt_hbm, seg_ref, high_hbm, low_hbm,
    back_hbm, fgrad_hbm,
    act_buf, grad_buf, filt_buf, high_buf, low_buf, spec_buf, grad_spec_buf, ret_buf, part_buf,
    in_send, in_recv, ret_send, ret_recv, part_send, part_recv, own_sem, load_sem, out_sem, fin_sem,
):
    me = lax.axis_index("seq")
    rep = lax.axis_index("rep")
    _, chans, toks = act_buf.shape
    length = seqs * toks
    bins = length
    rows = chans // chunks

    barrier = pltpu.get_barrier_semaphore()
    for dist in range(1, seqs):
        pl.semaphore_signal(
            barrier, inc=1, device_id={"seq": lax.rem(me + dist, seqs)}, device_id_type=MESH
        )
    for dist in range(1, reps):
        pl.semaphore_signal(
            barrier, inc=1, device_id={"rep": lax.rem(rep + dist, reps)}, device_id_type=MESH
        )

    loads = [
        pltpu.make_async_copy(filt_hbm, filt_buf, load_sem.at[0]),
        pltpu.make_async_copy(high_hbm, high_buf, load_sem.at[1]),
        pltpu.make_async_copy(low_hbm, low_buf, load_sem.at[2]),
    ]
    own = pl.ds(pl.multiple_of(me * chans, chans), chans)
    owns = [
        pltpu.make_async_copy(grad_hbm.at[own], grad_buf.at[me], own_sem.at[0]),
        pltpu.make_async_copy(act_hbm.at[own], act_buf.at[me], own_sem.at[1]),
    ]
    for copy in loads + owns:
        copy.start()

    pl.semaphore_wait(barrier, seqs - 1 + reps - 1)

    arrivals = []
    for chunk in range(chunks):
        for kind, (source, target) in enumerate(((grad_hbm, grad_buf), (act_hbm, act_buf))):
            group = []
            for dist in range(1, seqs):
                peer = lax.rem(me + dist, seqs)
                first = pl.multiple_of(peer * chans + chunk * rows, rows)
                copy = pltpu.make_async_remote_copy(
                    src_ref=source.at[pl.ds(first, rows)],
                    dst_ref=target.at[me, pl.ds(chunk * rows, rows)],
                    send_sem=in_send.at[chunk, kind, dist - 1],
                    recv_sem=in_recv.at[chunk, kind, dist - 1],
                    device_id={"seq": peer},
                    device_id_type=MESH,
                )
                copy.start()
                group.append(copy)
            arrivals.append(group)

    second = seg_ref[...].astype(jnp.float32)
    first_mask = 1.0 - second
    second_bf = second.astype(jnp.bfloat16)
    first_bf = first_mask.astype(jnp.bfloat16)

    for copy in loads:
        copy.wait()
    high, low = split(filt_buf[...])
    spec_buf[...] = triple(high, low, high_buf[...], low_buf[...], False)

    def pair_spectrum(buf, chunk):
        whole = jnp.concatenate(
            [buf[seq, pl.ds(chunk * rows, rows), :] for seq in range(seqs)], axis=1
        )
        high, low = split(whole)
        highs = jnp.concatenate([high * first_bf, high * second_bf], axis=0)
        lows = jnp.concatenate([low * first_bf, low * second_bf], axis=0)
        return triple(highs, lows, high_buf[...], low_buf[...], False)

    def inverse(spectrum):
        high, low = split(spectrum)
        return triple(high, low, high_buf[...], low_buf[...], True)

    returns = []
    for chunk in range(chunks):
        span = pl.ds(chunk * rows, rows)
        if chunk == 0:
            owns[0].wait()
        for copy in arrivals[2 * chunk]:
            copy.wait_recv()
        grad_spec = pair_spectrum(grad_buf, chunk)
        grad_spec_buf[chunk] = grad_spec
        filt_spec = spec_buf[span, :]
        both = jnp.concatenate(
            [conj_mul(filt_spec, grad_spec[:rows], bins), conj_mul(filt_spec, grad_spec[rows:], bins)],
            axis=0,
        )
        back = inverse(both)
        back = first_mask * back[:rows] + second * back[rows:]
        for seq in range(seqs):
            ret_buf[seq, span, :] = back[:, seq * toks : (seq + 1) * toks]
        target = pl.ds(pl.multiple_of(me * chans + chunk * rows, rows), rows)
        for dist in range(1, seqs):
            peer = lax.rem(me + dist, seqs)
            copy = pltpu.make_async_remote_copy(
                src_ref=ret_buf.at[peer, span],
                dst_ref=back_hbm.at[target],
                send_sem=ret_send.at[chunk, dist - 1],
                recv_sem=ret_recv.at[chunk, dist - 1],
                device_id={"seq": peer},
                device_id_type=MESH,
            )
            copy.start()
            returns.append(copy)
        keep = pltpu.make_async_copy(ret_buf.at[me, span], back_hbm.at[target], out_sem.at[chunk])
        keep.start()
        returns.append(keep)

        if chunk == 0:
            owns[1].wait()
        for copy in arrivals[2 * chunk + 1]:
            copy.wait_recv()
        act_spec = pair_spectrum(act_buf, chunk)
        grad_spec = grad_spec_buf[chunk]
        total = conj_mul(act_spec[:rows], grad_spec[:rows], bins) + conj_mul(
            act_spec[rows:], grad_spec[rows:], bins
        )
        part_buf[span, :] = inverse(total)
        for dist in range(1, reps):
            copy = pltpu.make_async_remote_copy(
                src_ref=part_buf.at[span],
                dst_ref=fgrad_hbm.at[rep, span],
                send_sem=part_send.at[chunk, dist - 1],
                recv_sem=part_recv.at[chunk, dist - 1],
                device_id={"rep": lax.rem(rep + dist, reps)},
                device_id_type=MESH,
            )
            copy.start()
            returns.append(copy)
        keep = pltpu.make_async_copy(part_buf.at[span], fgrad_hbm.at[rep, span], fin_sem.at[chunk])
        keep.start()
        returns.append(keep)

    for group in arrivals:
        for copy in group:
            copy.wait_send()
    for copy in returns:
        copy.wait()


def dense_body(inputs, out_grad, filters, segment_ids):
    seqs = lax.axis_size("seq")
    reps = lax.axis_size("rep")
    slab, toks = inputs.shape[1:]
    chans = slab // seqs
    length = seqs * toks
    chunks = CHUNKS
    rows = chans // chunks
    high, low = dense_table(length)
    remote = pl.BlockSpec(memory_space=pltpu.HBM)
    vmem = pl.BlockSpec(memory_space=pltpu.VMEM)
    f32, bf16, dma = jnp.float32, jnp.bfloat16, pltpu.SemaphoreType.DMA
    back, fgrad = pl.pallas_call(
        functools.partial(kernel, seqs, reps, chunks),
        out_shape=(
            pltpu.VMEM((slab, toks), f32),
            pltpu.VMEM((reps, chans, length), f32),
        ),
        in_specs=[remote] * 3 + [vmem] + [remote] * 2,
        out_specs=(vmem, vmem),
        scratch_shapes=[
            pltpu.VMEM((seqs, chans, toks), f32),
            pltpu.VMEM((seqs, chans, toks), f32),
            pltpu.VMEM((chans, length), f32),
            pltpu.VMEM((length, 2 * length), bf16),
            pltpu.VMEM((length, 2 * length), bf16),
            pltpu.VMEM((chans, 2 * length), f32),
            pltpu.VMEM((chunks, 2 * rows, 2 * length), f32),
            pltpu.VMEM((seqs, chans, toks), f32),
            pltpu.VMEM((chans, length), f32),
            dma((chunks, 2, seqs - 1)),
            dma((chunks, 2, seqs - 1)),
            dma((chunks, seqs - 1)),
            dma((chunks, seqs - 1)),
            dma((chunks, reps - 1)),
            dma((chunks, reps - 1)),
            dma((2,)),
            dma((3,)),
            dma((chunks,)),
            dma((chunks,)),
        ],
        compiler_params=pltpu.CompilerParams(
            collective_id=0, has_side_effects=True, vmem_limit_bytes=60000 * 1024
        ),
    )(inputs[0], out_grad[0], filters[0], segment_ids, jnp.asarray(high), jnp.asarray(low))
    factor = 1.0 / length
    total = fgrad[0]
    for other in range(1, reps):
        total = total + fgrad[other]
    return (back * factor)[None], (total * factor)[None]


def body(inputs, out_grad, filters, segment_ids):
    length = filters.shape[2]
    if length * 2 * length * 4 <= TABLE_BYTES:
        return dense_body(inputs, out_grad, filters, segment_ids)
    return long_body(inputs, out_grad, filters, segment_ids)


def solution(mesh):
    return jax.shard_map(
        body,
        mesh=mesh,
        in_specs=(
            P("rep", "chan", "seq"),
            P("rep", "chan", "seq"),
            P("chan", "seq", None),
            P("rep", None),
        ),
        out_specs=(P("rep", "chan", "seq"), P("chan", "seq", None)),
        check_vma=False,
    )
```

```python
import functools
import math

import jax
import jax.numpy as jnp
import numpy as np
from jax import lax
from jax.experimental import pallas as pl
from jax.experimental.pallas import tpu as pltpu
from jax.sharding import PartitionSpec as P

MESH = pl.DeviceIdType.MESH
TABLE_BYTES = 8 << 20
WEIGHTS = (2, 1, 1)


def table_pair(row_count, col_count, period):
    row_index = jnp.arange(row_count, dtype=jnp.int32)[:, None]
    col_index = jnp.arange(col_count, dtype=jnp.int32)[None, :]
    phases = row_index * col_index % period
    angles = phases.astype(jnp.float32) * (2.0 * math.pi / period)
    return (jnp.cos(angles), -jnp.sin(angles))


def contract(formula, left_part, right_part):
    return jnp.einsum(
        formula,
        left_part,
        right_part,
        precision=lax.Precision.HIGHEST,
        preferred_element_type=jnp.float32,
    )


def make_tables(length):
    full_len = 2 * length
    col_size = 128
    row_size = full_len // col_size
    half_rows = row_size // 2
    outer_cos, outer_sin = table_pair(row_size, row_size, row_size)
    fwd_cos = outer_cos[:, :half_rows]
    fwd_sin = outer_sin[:, :half_rows]
    outer_fwd = jnp.concatenate(
        [jnp.concatenate([fwd_cos, -fwd_sin], axis=1), jnp.concatenate([fwd_sin, fwd_cos], axis=1)],
        axis=0,
    )
    inv_cos = outer_cos[:half_rows]
    inv_sin = outer_sin[:half_rows]
    outer_inv = jnp.concatenate(
        [jnp.concatenate([inv_cos, inv_sin], axis=1), jnp.concatenate([-inv_sin, inv_cos], axis=1)],
        axis=0,
    )
    twiddle = table_pair(row_size, col_size, full_len)
    inner_cos, inner_sin = table_pair(col_size, col_size, col_size)
    inner_fwd = jnp.stack(
        [jnp.stack([inner_cos, inner_sin], axis=1), jnp.stack([-inner_sin, inner_cos], axis=1)],
        axis=0,
    )
    inner_inv = jnp.stack(
        [jnp.stack([inner_cos, -inner_sin], axis=1), jnp.stack([inner_sin, inner_cos], axis=1)],
        axis=0,
    )
    return (outer_fwd, outer_inv, twiddle, inner_fwd, inner_inv, half_rows, col_size)


def forward_spectrum(signal, real_only, tables):
    outer_fwd, outer_inv, twiddle, inner_fwd, inner_inv, half_rows, col_size = tables
    chan_count = signal.shape[0]
    if real_only:
        section = contract("ja,cab->cjb", outer_fwd[:, :half_rows], signal)
    else:
        section = contract(
            "ja,cab->cjb", outer_fwd, signal.reshape(chan_count, 2 * half_rows, col_size)
        )
    section = section.reshape(chan_count, 2, 2 * half_rows, col_size)
    section_re = section[:, 0]
    section_im = section[:, 1]
    turned = jnp.stack(
        [
            section_re * twiddle[0] - section_im * twiddle[1],
            section_re * twiddle[1] + section_im * twiddle[0],
        ],
        axis=1,
    )
    return contract("cpjb,pbqm->cqjm", turned, inner_fwd)


def inverse_signal(spectrum, tables, want_imag):
    outer_fwd, outer_inv, twiddle, inner_fwd, inner_inv, half_rows, col_size = tables
    chan_count = spectrum.shape[0]
    factor = 1.0 / (2 * half_rows * col_size)
    mixed = contract("cqjm,qmpb->cpjb", spectrum, inner_inv)
    mixed_re = mixed[:, 0]
    mixed_im = mixed[:, 1]
    turned = jnp.stack(
        [
            mixed_re * twiddle[0] + mixed_im * twiddle[1],
            mixed_im * twiddle[0] - mixed_re * twiddle[1],
        ],
        axis=1,
    )
    turned = turned.reshape(chan_count, 4 * half_rows, col_size)
    table = outer_inv if want_imag else outer_inv[:half_rows]
    signal = contract("aj,cjb->cab", table, turned) * factor
    return signal.reshape(chan_count, -1, half_rows, col_size)


def conj_product(left_spec, right_spec):
    left_re = left_spec[:, 0]
    left_im = left_spec[:, 1]
    right_re = right_spec[:, 0]
    right_im = right_spec[:, 1]
    return jnp.stack(
        [left_re * right_re + left_im * right_im, left_re * right_im - left_im * right_re], axis=1
    )


def pair_spectrum(whole, first_mask, second_mask, tables):
    signal = whole.reshape(-1, tables[5], tables[6])
    packed = jnp.stack([signal * first_mask, signal * second_mask], axis=1)
    return forward_spectrum(packed, False, tables)


def return_grad(filter_spec, grad_spec, first_mask, second_mask, tables, slab_width, tok_count):
    product = conj_product(filter_spec, grad_spec)
    back = inverse_signal(product, tables, True)
    grad_full = first_mask * back[:, 0] + second_mask * back[:, 1]
    chan_count = grad_full.shape[0]
    pieces = grad_full.reshape(1, chan_count, -1)
    returned = lax.all_to_all(pieces, "seq", split_axis=2, concat_axis=0, tiled=True)
    return returned.reshape(1, slab_width, tok_count)


def sum_filter_grad(act_spec, grad_spec, tables):
    product = conj_product(act_spec, grad_spec)
    signal_re = inverse_signal(product, tables, False)
    chan_count = signal_re.shape[0]
    return lax.psum(signal_re.reshape(1, chan_count, -1), "rep")


def long_body(inputs, out_grad, filters, segment_ids):
    seq_count = lax.axis_size("seq")
    slab_width = inputs.shape[1]
    tok_count = inputs.shape[2]
    chan_count = slab_width // seq_count
    length = tok_count * seq_count
    tables = make_tables(length)
    half_rows = tables[5]
    col_size = tables[6]
    second_mask = segment_ids[0].astype(jnp.float32).reshape(half_rows, col_size)
    first_mask = 1.0 - second_mask
    filter_spec = forward_spectrum(
        filters[0].reshape(chan_count, half_rows, col_size), True, tables
    )
    act_pieces = inputs.reshape(seq_count, chan_count, tok_count)
    grad_pieces = out_grad.reshape(seq_count, chan_count, tok_count)
    act_whole, grad_whole = (
        lax.all_to_all(act_pieces, "seq", split_axis=0, concat_axis=2, tiled=True),
        lax.all_to_all(grad_pieces, "seq", split_axis=0, concat_axis=2, tiled=True),
    )
    grad_spec = pair_spectrum(grad_whole, first_mask, second_mask, tables)
    input_grad = return_grad(
        filter_spec, grad_spec, first_mask, second_mask, tables, slab_width, tok_count
    )
    act_spec = pair_spectrum(act_whole, first_mask, second_mask, tables)
    filter_grad = sum_filter_grad(act_spec, grad_spec, tables)
    return (input_grad, filter_grad)


def dense_table(length):
    phase = np.arange(length)[:, None] * (2 * np.arange(length)[None, :] + 1) % (4 * length)
    angle = phase * (math.pi / (2 * length))
    table = np.concatenate([np.cos(angle), -np.sin(angle)], axis=1).astype(np.float32)
    high = table.astype(jnp.bfloat16)
    low = (table - high.astype(np.float32)).astype(jnp.bfloat16)
    return high, low


def split(value):
    high = value.astype(jnp.bfloat16)
    low = (value - high.astype(jnp.float32)).astype(jnp.bfloat16)
    return high, low


def dot(left, right, inverse):
    dims = (((1,), (1 if inverse else 0,)), ((), ()))
    return lax.dot_general(left, right, dims, preferred_element_type=jnp.float32)


def triple(high, low, high_table, low_table, inverse):
    return dot(high, high_table, inverse) + (
        dot(low, high_table, inverse) + dot(high, low_table, inverse)
    )


def conj_mul(left, right, bins):
    left_re, left_im = left[:, :bins], left[:, bins:]
    right_re, right_im = right[:, :bins], right[:, bins:]
    return jnp.concatenate(
        [left_re * right_re + left_im * right_im, left_re * right_im - left_im * right_re], axis=1
    )


def kernel(
    seqs, reps, chunks,
    act_hbm, grad_hbm, filt_hbm, seg_ref, high_hbm, low_hbm,
    back_hbm, fgrad_hbm,
    act_buf, grad_buf, filt_buf, high_buf, low_buf, spec_buf, ret_buf, part_buf,
    in_send, in_recv, ret_send, ret_recv, part_send, part_recv, own_sem, load_sem, out_sem,
):
    me = lax.axis_index("seq")
    rep = lax.axis_index("rep")
    _, chans, toks = act_buf.shape
    length = seqs * toks
    bins = length
    edges = [chans * sum(WEIGHTS[:chunk]) // sum(WEIGHTS) for chunk in range(chunks + 1)]

    barrier = pltpu.get_barrier_semaphore()
    for dist in range(1, seqs):
        pl.semaphore_signal(
            barrier, inc=1, device_id={"seq": lax.rem(me + dist, seqs)}, device_id_type=MESH
        )
    for dist in range(1, reps):
        pl.semaphore_signal(
            barrier, inc=1, device_id={"rep": lax.rem(rep + dist, reps)}, device_id_type=MESH
        )

    loads = [
        pltpu.make_async_copy(filt_hbm, filt_buf, load_sem.at[0]),
        pltpu.make_async_copy(high_hbm, high_buf, load_sem.at[1]),
        pltpu.make_async_copy(low_hbm, low_buf, load_sem.at[2]),
    ]
    own = pl.ds(pl.multiple_of(me * chans, chans), chans)
    owns = [
        pltpu.make_async_copy(grad_hbm.at[own], grad_buf.at[me], own_sem.at[0]),
        pltpu.make_async_copy(act_hbm.at[own], act_buf.at[me], own_sem.at[1]),
    ]
    for copy in loads + owns:
        copy.start()

    pl.semaphore_wait(barrier, seqs - 1 + reps - 1)

    arrivals = []
    for chunk in range(chunks):
        for kind, (source, target) in enumerate(((grad_hbm, grad_buf), (act_hbm, act_buf))):
            group = []
            rows = edges[chunk + 1] - edges[chunk]
            for dist in range(1, seqs):
                peer = lax.rem(me + dist, seqs)
                first = pl.multiple_of(peer * chans + edges[chunk], 8)
                copy = pltpu.make_async_remote_copy(
                    src_ref=source.at[pl.ds(first, rows)],
                    dst_ref=target.at[me, pl.ds(edges[chunk], rows)],
                    send_sem=in_send.at[chunk, kind, dist - 1],
                    recv_sem=in_recv.at[chunk, kind, dist - 1],
                    device_id={"seq": peer},
                    device_id_type=MESH,
                )
                copy.start()
                group.append(copy)
            arrivals.append(group)

    second = seg_ref[...].astype(jnp.float32)
    first_mask = 1.0 - second
    second_bf = second.astype(jnp.bfloat16)
    first_bf = first_mask.astype(jnp.bfloat16)

    for copy in loads:
        copy.wait()
    high, low = split(filt_buf[...])
    spec_buf[...] = triple(high, low, high_buf[...], low_buf[...], False)

    def pair_spectrum(buf, span):
        whole = jnp.concatenate(
            [buf[seq, span, :] for seq in range(seqs)], axis=1
        )
        high, low = split(whole)
        highs = jnp.concatenate([high * first_bf, high * second_bf], axis=0)
        lows = jnp.concatenate([low * first_bf, low * second_bf], axis=0)
        return triple(highs, lows, high_buf[...], low_buf[...], False)

    def inverse(spectrum):
        high, low = split(spectrum)
        return triple(high, low, high_buf[...], low_buf[...], True) * (1.0 / length)

    returns = []
    parts = []
    for chunk in range(chunks):
        rows = edges[chunk + 1] - edges[chunk]
        span = pl.ds(edges[chunk], rows)
        if chunk == 0:
            owns[0].wait()
        for copy in arrivals[2 * chunk]:
            copy.wait_recv()
        grad_spec = pair_spectrum(grad_buf, span)
        filt_spec = spec_buf[span, :]
        both = jnp.concatenate(
            [conj_mul(filt_spec, grad_spec[:rows], bins), conj_mul(filt_spec, grad_spec[rows:], bins)],
            axis=0,
        )
        back = inverse(both)
        back = first_mask * back[:rows] + second * back[rows:]
        for seq in range(seqs):
            ret_buf[seq, span, :] = back[:, seq * toks : (seq + 1) * toks]
        target = pl.ds(pl.multiple_of(me * chans + edges[chunk], 8), rows)
        for dist in range(1, seqs):
            peer = lax.rem(me + dist, seqs)
            copy = pltpu.make_async_remote_copy(
                src_ref=ret_buf.at[peer, span],
                dst_ref=back_hbm.at[target],
                send_sem=ret_send.at[chunk, dist - 1],
                recv_sem=ret_recv.at[chunk, dist - 1],
                device_id={"seq": peer},
                device_id_type=MESH,
            )
            copy.start()
            returns.append(copy)
        keep = pltpu.make_async_copy(ret_buf.at[me, span], back_hbm.at[target], out_sem.at[chunk])
        keep.start()
        returns.append(keep)

        if chunk == 0:
            owns[1].wait()
        for copy in arrivals[2 * chunk + 1]:
            copy.wait_recv()
        act_spec = pair_spectrum(act_buf, span)
        total = conj_mul(act_spec[:rows], grad_spec[:rows], bins) + conj_mul(
            act_spec[rows:], grad_spec[rows:], bins
        )
        part_buf[rep, span, :] = inverse(total)
        for dist in range(1, reps):
            copy = pltpu.make_async_remote_copy(
                src_ref=part_buf.at[rep, span],
                dst_ref=part_buf.at[rep, span],
                send_sem=part_send.at[chunk, dist - 1],
                recv_sem=part_recv.at[chunk, dist - 1],
                device_id={"rep": lax.rem(rep + dist, reps)},
                device_id_type=MESH,
            )
            copy.start()
            parts.append(copy)

    for copy in parts:
        copy.wait()
    total = part_buf[0]
    for other in range(1, reps):
        total = total + part_buf[other]
    fgrad_hbm[...] = total
    for group in arrivals:
        for copy in group:
            copy.wait_send()
    for copy in returns:
        copy.wait()


def dense_body(inputs, out_grad, filters, segment_ids):
    seqs = lax.axis_size("seq")
    reps = lax.axis_size("rep")
    slab, toks = inputs.shape[1:]
    chans = slab // seqs
    length = seqs * toks
    chunks = len(WEIGHTS)
    high, low = dense_table(length)
    remote = pl.BlockSpec(memory_space=pltpu.HBM)
    vmem = pl.BlockSpec(memory_space=pltpu.VMEM)
    f32, bf16, dma = jnp.float32, jnp.bfloat16, pltpu.SemaphoreType.DMA
    back, fgrad = pl.pallas_call(
        functools.partial(kernel, seqs, reps, chunks),
        out_shape=(
            pltpu.VMEM((slab, toks), f32),
            pltpu.VMEM((chans, length), f32),
        ),
        in_specs=[remote] * 3 + [vmem] + [remote] * 2,
        out_specs=(vmem, vmem),
        scratch_shapes=[
            pltpu.VMEM((seqs, chans, toks), f32),
            pltpu.VMEM((seqs, chans, toks), f32),
            pltpu.VMEM((chans, length), f32),
            pltpu.VMEM((length, 2 * length), bf16),
            pltpu.VMEM((length, 2 * length), bf16),
            pltpu.VMEM((chans, 2 * length), f32),
            pltpu.VMEM((seqs, chans, toks), f32),
            pltpu.VMEM((reps, chans, length), f32),
            dma((chunks, 2, seqs - 1)),
            dma((chunks, 2, seqs - 1)),
            dma((chunks, seqs - 1)),
            dma((chunks, seqs - 1)),
            dma((chunks, reps - 1)),
            dma((chunks, reps - 1)),
            dma((2,)),
            dma((3,)),
            dma((chunks,)),
        ],
        compiler_params=pltpu.CompilerParams(
            collective_id=0, has_side_effects=True, vmem_limit_bytes=60000 * 1024
        ),
    )(inputs[0], out_grad[0], filters[0], segment_ids, jnp.asarray(high), jnp.asarray(low))
    return back[None], fgrad[None]


def body(inputs, out_grad, filters, segment_ids):
    length = filters.shape[2]
    if length * 2 * length * 4 <= TABLE_BYTES:
        return dense_body(inputs, out_grad, filters, segment_ids)
    return long_body(inputs, out_grad, filters, segment_ids)


def solution(mesh):
    return jax.shard_map(
        body,
        mesh=mesh,
        in_specs=(
            P("rep", "chan", "seq"),
            P("rep", "chan", "seq"),
            P("chan", "seq", None),
            P("rep", None),
        ),
        out_specs=(P("rep", "chan", "seq"), P("chan", "seq", None)),
        check_vma=False,
    )
```
